256 devices in a mesh: ctx: 8 (over x, y_lo), chan: 32 (over y_hi, z, core).
Axes of the slice: x: 4, y: 4 (y_hi: 2, y_lo: 2; y = y_hi * 2 + y_lo), z: 8, core: 2. Of those that a mesh axis runs over, the one named last changes fastest.
Arguments:
- tokens: bfloat16 [4096, 8192], P('ctx', 'chan'), may hold values from -6 to 6
- in_base: bfloat16 [8192, 3, 4096], P('ctx', None, 'chan'), may hold values from -0.0625 to 0.0625
- in_task: bfloat16 [8192, 3, 4096], P('ctx', None, 'chan'), may hold values from -0.03125 to 0.03125
- feat_weight: float32 [7, 3, 4096], P(None, None, 'chan'), may hold values from -2 to 2
- filter_taps: float32 [128, 4096], P(None, 'chan'), may hold values from -0.5 to 0.5
- decay_rates: float32 [4096], P('chan'), may hold values from 0.002 to 0.08
- skip_gain: float32 [4096], P('chan'), may hold values from -1 to 1
- out_base: bfloat16 [4096, 8192], P('chan', 'ctx'), may hold values from -0.1875 to 0.1875
- out_task: bfloat16 [4096, 8192], P('chan', 'ctx'), may hold values from -0.046875 to 0.046875
Outputs:
- layer_out: bfloat16 [4096, 8192], P('ctx', 'chan')
The draws below stay inside these ranges and needn't reach their ends.
All inputs are finite; a program needn't handle non-finite values.
Results may differ from the reference program's by a relative error of at most 0.0092.
Values may be sent and summed in bfloat16 or wider, within the bound.
A program may use at most 128 MiB of HBM per device.

```python
import math
import jax
import jax.numpy as jnp
from jax import lax

D = 8192
H = 4096
FLT = 128
FEAT = 7
TOKENS = 4096


def with_spikes(array, own_key, source, target, parts, factor):
    def block_of(position):
        return (jnp.arange(array.shape[position]) // (array.shape[position] // parts)).reshape((-1,) + (1,) * (array.ndim - 1 - position))

    first = jax.random.permutation(own_key, parts)[block_of(target)]
    second = (block_of(target) + parts // 2) % parts
    return jnp.where((block_of(source) == first) | (block_of(source) == second), factor * array, array)


def shard_levels(stream_key, shape, pieces, smallest, high):
    factor_of = 1.0
    for position, parts in pieces:
        draws = jax.random.uniform(jax.random.fold_in(jax.random.fold_in(stream_key, 6), position), (parts,), jnp.float32, smallest / len(pieces), high / len(pieces))
        factor_of = factor_of * jnp.repeat(jnp.exp(draws), shape[position] // parts).reshape((-1,) + (1,) * (len(shape) - 1 - position))
    return factor_of


def scatter_about(rng, dims, width, bound, pieces=(), kind=jnp.bfloat16):
    entries = width * jax.random.normal(rng, dims, jnp.float32)
    if pieces:
        entries = entries * shard_levels(rng, dims, pieces, -0.22, 0.18)
    return jnp.clip(entries, -bound, bound).astype(kind)


def noise_with(own_key, shape, deviation, limit, cuts, heavy, kind=jnp.bfloat16):
    values = deviation * jax.random.normal(own_key, shape, jnp.float32)
    if cuts:
        values = values * shard_levels(own_key, shape, cuts, -0.22, 0.18)
    return jnp.clip(with_spikes(values, jax.random.fold_in(own_key, 3), *heavy), -limit, limit).astype(kind)


def setup_inputs(seed: int = 0) -> dict:
    seeds = jax.random.split(jax.random.key(seed), 10)
    tokens = scatter_about(seeds[0], (TOKENS, D), 1.0, 6.0, ((0, 8), (1, 32)))
    in_base = scatter_about(seeds[1], (D, 3, H), D ** -0.5, 0.0625, ((0, 8), (2, 32)))
    in_task = scatter_about(seeds[2], (D, 3, H), (4 * D) ** -0.5, 0.03125, ((0, 8), (2, 32)))
    feat_weight = scatter_about(seeds[3], (FEAT, 3, H), FEAT ** -0.5, 2.0, ((2, 32),), jnp.float32)
    filter_taps = scatter_about(seeds[4], (FLT, H), FLT ** -0.5, 0.5, ((1, 32),), jnp.float32)
    decay_rates = jnp.clip(jnp.exp(math.log(0.08) - 3.6888794 * jax.random.uniform(seeds[5], (H,), jnp.float32) ** shard_levels(seeds[5], (H,), ((0, 32),), -0.2, 0.2)), 0.002, 0.08)
    skip_gain = jnp.clip(jax.random.uniform(seeds[6], (H,), jnp.float32, -1.0, 1.0) * shard_levels(seeds[6], (H,), ((0, 32),), -0.4, 0.0), -1.0, 1.0)
    out_base = noise_with(seeds[7], (H, D), H ** -0.5, 0.1875, ((0, 32), (1, 8)), (0, 1, 32, 2.75))
    out_task = scatter_about(seeds[8], (H, D), (4 * H) ** -0.5, 0.046875, ((0, 32), (1, 8)))
    return {"tokens": tokens, "in_base": in_base, "in_task": in_task, "feat_weight": feat_weight, "filter_taps": filter_taps, "decay_rates": decay_rates, "skip_gain": skip_gain, "out_base": out_base, "out_task": out_task}


def featurize(projected, feat_weight):
    length = projected.shape[0]
    padded = jnp.pad(projected.astype(jnp.float32), ((FEAT - 1, 0), (0, 0), (0, 0)))
    result = jnp.zeros(projected.shape, jnp.float32)
    for offset in range(FEAT):
        result = result + feat_weight[offset] * padded[FEAT - 1 - offset:FEAT - 1 - offset + length]
    return result


def reference(tokens, in_base, in_task, feat_weight, filter_taps, decay_rates, skip_gain, out_base, out_task):
    in_weight = (in_base.astype(jnp.float32) - in_task.astype(jnp.float32)).astype(jnp.bfloat16)
    out_weight = (out_base.astype(jnp.float32) - out_task.astype(jnp.float32)).astype(jnp.bfloat16)
    length = tokens.shape[0]
    projected = jnp.dot(tokens, in_weight.reshape(D, 3 * H), preferred_element_type=jnp.float32)
    projected = projected.astype(jnp.bfloat16).reshape(length, 3, H)
    featured = featurize(projected, feat_weight)
    gated_input = featured[:, 1, :] * featured[:, 2, :]
    lag_values = jnp.arange(FLT, dtype=jnp.float32)
    filter_full = filter_taps * jnp.exp(-decay_rates[None, :] * lag_values[:, None])
    padded = jnp.pad(gated_input, ((FLT - 1, 0), (0, 0)))

    def add_tap(lag_index, running):
        shifted = lax.dynamic_slice_in_dim(padded, (FLT - 1 - lag_index).astype(jnp.int32), length, 0)
        return running + filter_full[lag_index] * shifted

    conv_sum = lax.fori_loop(jnp.int32(0), jnp.int32(FLT), add_tap, jnp.zeros((length, H), jnp.float32))
    mixed = skip_gain * gated_input + conv_sum
    gated_out = (featured[:, 0, :] * mixed).astype(jnp.bfloat16)
    summed = jnp.dot(gated_out, out_weight, preferred_element_type=jnp.float32)
    return summed.astype(jnp.bfloat16)
```

```python
import functools

import jax
import jax.numpy as jnp
from jax import lax
from jax.experimental import pallas as pl
from jax.experimental.pallas import tpu as pltpu
from jax.sharding import PartitionSpec as P

MESH = pl.DeviceIdType.MESH
NX, NZ = 4, 8
NCTX = 2 * NX
NQ = 2 * NZ
HALO = 144
bf16, f32 = jnp.bfloat16, jnp.float32


def kernel(
    rows, width, chans, short, longt,
    tok_ref, w_ref, wo_ref, feat_ref, taps_ref, decay_ref, skip_ref,
    out_ref,
    tok_all, w_all, wo_all, acc, part_in, halo_out, halo_in, proj, gate, shifts, query, filt,
    gated, msg_out, msg_in, y_out, y_in, total,
    send_sems, recv_sems, local_sems,
):
    ctx, chan = lax.axis_index("ctx"), lax.axis_index("chan")
    x, yl = ctx // 2, ctx % 2
    q, core = chan // 2, chan % 2
    yh, z = q // NZ, q % NZ
    c3 = 3 * chans

    def x_at(d):
        return ((x + d + NX) % NX) * 2 + yl, chan

    def z_at(d):
        return ctx, (yh * NZ + (z + d + NZ) % NZ) * 2 + core

    y_pair = (x * 2 + 1 - yl, chan)
    y_far = (ctx, ((1 - yh) * NZ + z) * 2 + core)
    twin = (ctx, 2 * q + 1 - core)
    after, before = ((ctx + 1) % NCTX, chan), ((ctx + NCTX - 1) % NCTX, chan)

    barrier = pltpu.get_barrier_semaphore()
    greeted = [twin, y_pair, y_far, x_at(1), x_at(-1), z_at(1), z_at(-1), after, before]
    for device in greeted:
        pl.semaphore_signal(barrier, inc=1, device_id=device, device_id_type=MESH)
    pl.semaphore_wait(barrier, len(greeted))

    copies = {}

    def send(name, src, dst, device):
        k = len(copies)
        copy = pltpu.make_async_remote_copy(
            src_ref=src, dst_ref=dst, send_sem=send_sems.at[k], recv_sem=recv_sems.at[k],
            device_id=device, device_id_type=MESH,
        )
        copy.start()
        copies[name] = copy

    def arrived(name):
        copies[name].wait_recv()

    def w_at(i, h):
        return w_all.at[pl.ds(2 * i, 2), :, pl.ds(h * c3, c3)]

    def wo_at(i, h):
        return wo_all.at[pl.ds(2 * i, 2), pl.ds(h * chans, chans), :]

    def ctx_of(d, other):
        return ((x + d + NX) % NX) * 2 + (1 - yl if other else yl)

    def tok_at(d, other):
        return tok_all.at[(1 - yh if other else yh) * NZ + (z + d + NZ) % NZ]

    send("twin_w", w_ref.at[:, 1 - core], w_at(ctx, 1), twin)
    for d in (1, -1):
        send(("tok", 0, d, 1), tok_ref, tok_at(0, 0), z_at(d))
    send("tok_y", tok_ref, tok_at(0, 0), y_far)
    for d in (1, -1):
        send(("w", 0, 0, d), w_ref.at[:, core], w_at(ctx, 0), x_at(d))
    send(("wy", 0), w_ref.at[:, core], w_at(ctx, 0), y_pair)
    send("twin_wo", wo_ref.at[:, 1 - core], wo_at(ctx, 1), twin)
    local = [
        pltpu.make_async_copy(w_ref.at[:, core], w_at(ctx, 0), local_sems.at[0]),
        pltpu.make_async_copy(wo_ref.at[:, core], wo_at(ctx, 0), local_sems.at[1]),
        pltpu.make_async_copy(tok_ref, tok_at(0, 0), local_sems.at[2]),
    ]
    for copy in local:
        copy.start()

    arrived("twin_w")
    for d in (1, -1):
        send(("w", 0, 1, d), w_at(ctx, 1), w_at(ctx, 1), x_at(d))
    send(("wy", 1), w_at(ctx, 1), w_at(ctx, 1), y_pair)
    for copy in local:
        copy.wait()
    arrived("twin_wo")
    for h in (0, 1):
        send(("woy", 0, h), wo_at(ctx, h), wo_at(ctx, h), y_pair)

    lags = lax.broadcasted_iota(jnp.int32, (longt, chans), 0).astype(f32)
    filt[...] = taps_ref[...] * jnp.exp(-decay_ref[...] * lags)
    acc[...] = jnp.zeros_like(acc)

    half = rows // 2

    def tok_step(o, step):
        for d in (1, -1):
            if step == 1:
                if not o:
                    continue
                src = tok_at(0, 1)
            else:
                arrived(("tok", o, d, step - 1))
                src = tok_at(-d * (step - 1), o)
            if step == NZ // 2:
                src = src.at[pl.ds(0 if d == 1 else half, half)]
            send(("tok", o, d, step), src, src, z_at(d))

    def w_pass(o):
        for d, h in ((1, 0), (-1, 1)):
            arrived(("w", o, h, d))
            src = w_at(ctx_of(-d, o), h)
            send(("w_far", o, d), src, src, x_at(d))

    def w_second(h):
        arrived(("wy", h))
        for d in (1, -1):
            src = w_at(ctx_of(0, 1), h)
            send(("w", 1, h, d), src, src, x_at(d))

    arrived("tok_y")
    tok_step(1, 1)
    tok_step(0, 2)
    w_second(0)
    tok_step(1, 2)
    tok_step(0, 3)
    w_second(1)
    w_pass(0)
    tok_step(1, 3)
    tok_step(0, 4)
    tok_step(1, 4)
    w_pass(1)
    for h in (0, 1):
        for d in (1, -1):
            send(("wo", h, d), wo_at(ctx, h), wo_at(ctx, h), x_at(d))
    for o in (0, 1):
        for d in (1, -1):
            arrived(("tok", o, d, NZ // 2))
            arrived(("w", o, 1 if d == 1 else 0, d))

    def accumulate(k, first, size):
        i = ((x + k // 2 + NX - 1) % NX) * 2 + k % 2
        cols = pl.ds(first, size)
        for r in range(2):
            band = pl.ds(r * half, half)
            acc[band, cols] += jnp.dot(
                tok_all[2 * i, band, :], w_all[2 * i, :, cols], preferred_element_type=f32
            ) + jnp.dot(
                tok_all[2 * i + 1, band, :], w_all[2 * i + 1, :, cols], preferred_element_type=f32
            )

    @pl.loop(0, 2 * NX - 2)
    def _(k):
        accumulate(k, 0, 2 * c3)

    for o in (0, 1):
        for d in (1, -1):
            arrived(("w_far", o, d))

    @pl.loop(2 * NX - 2, 2 * NX)
    def _(k):
        accumulate(k, c3, c3)

    send("part", acc.at[:, pl.ds(c3, c3)], part_in, twin)

    @pl.loop(2 * NX - 2, 2 * NX)
    def _(k):
        accumulate(k, 0, c3)

    for d in (1, -1):
        for h in (0, 1):
            arrived(("wo", h, d))
            src = wo_at(ctx_of(-d, 0), h)
            send(("woy", d, h), src, src, y_pair)
        src = wo_at(ctx_of(-d, 0), 0 if d == 1 else 1)
        send(("wo_far", d), src, src, x_at(d))

    arrived("part")
    last = pl.ds(rows - HALO, HALO)
    tail = (acc[last, pl.ds(0, c3)] + part_in[last, :]).astype(bf16)
    halo_out[...] = tail
    proj[pl.ds(rows, HALO), :] = tail.astype(f32)
    step_rows = (rows - HALO) // 2

    @pl.loop(0, 2)
    def _(k):
        at = pl.multiple_of(k * step_rows, 8)
        mine = (acc[pl.ds(at, step_rows), pl.ds(0, c3)] + part_in[pl.ds(at, step_rows), :]).astype(bf16)
        proj[pl.ds(pl.multiple_of(at + HALO, 8), step_rows), :] = mine.astype(f32)

    send("halo", halo_out, halo_in, after)

    def featurize(begin, count, with_query):
        size = 32

        @pl.loop(0, count // size)
        def _(k):
            at = pl.multiple_of(begin + k * size, 8)
            values = []
            for s in range(3):
                if s == 0 and not with_query:
                    values.append(None)
                    continue
                lanes = pl.ds(s * chans, chans)
                block = proj[pl.ds(pl.multiple_of(at - 8, 8), size + 8), lanes]
                value = feat_ref[0:1, lanes] * block[8:]
                for i in range(1, short):
                    value += feat_ref[i : i + 1, lanes] * block[8 - i : 8 - i + size]
                values.append(value)
            gate[pl.ds(at, size), :] = values[1] * values[2]
            if with_query:
                query[pl.ds(pl.multiple_of(at - HALO, 8), size), :] = values[0]

    def shift(begin, count):
        size = 32

        @pl.loop(0, count // size)
        def _(k):
            at = pl.multiple_of(begin + k * size, 8)
            block = gate[pl.ds(pl.multiple_of(at - 8, 8), size + 8), :]
            for r in range(8):
                shifts[r, pl.ds(at, size), :] = block[8 - r : 8 - r + size]

    tile = 64

    def convolve(begin, count):
        @pl.loop(begin, begin + count)
        def _(k):
            at = pl.multiple_of(k * tile, tile)
            own = shifts[0, pl.ds(pl.multiple_of(at + HALO, 8), tile), :]
            value = skip_ref[...] * own
            for j in range(longt):
                back, r = j - j % 8, j % 8
                value += filt[j : j + 1, :] * shifts[r, pl.ds(pl.multiple_of(at + HALO - back, 8), tile), :]
            gated[pl.ds(at, tile), pl.ds(0, chans)] = (query[pl.ds(at, tile), :] * value).astype(bf16)

    tiles = rows // tile
    first_free = 3
    featurize(HALO + 32, rows - 32, True)
    shift(HALO + 48, rows - 64)
    shift(HALO + rows - 32, 32)
    convolve(first_free, tiles - first_free)
    band = pl.ds(first_free * tile, rows - first_free * tile)
    send("gated_hi", gated.at[band, pl.ds(0, chans)], gated.at[band, pl.ds(chans, chans)], twin)

    for d in (1, -1):
        arrived(("wo_far", d))
        src = wo_at(ctx_of(2, 0), 0 if d == 1 else 1)
        send(("woy_far", d), src, src, y_pair)

    arrived("halo")
    proj[pl.ds(0, HALO), :] = jnp.where(ctx == 0, 0.0, halo_in[...].astype(f32))
    featurize(16, HALO - 16, False)
    featurize(HALO, 32, True)
    shift(24, HALO + 48)
    convolve(0, first_free)
    band = pl.ds(0, first_free * tile)
    send("gated_lo", gated.at[band, pl.ds(0, chans)], gated.at[band, pl.ds(chans, chans)], twin)
    for d in (1, -1):
        for h in (0, 1):
            arrived(("woy", d, h))
        arrived(("woy_far", d))
    for h in (0, 1):
        arrived(("woy", 0, h))
    arrived("gated_hi")
    arrived("gated_lo")

    piece = 128

    def partial(at, d, other):
        to = (1 - yh if other else yh) * NZ + (z + d + NZ) % NZ
        return jnp.dot(gated[pl.ds(at, piece), :], wo_all[to], preferred_element_type=f32)

    def message(s, j, other):
        d = 1 if s == 0 else -1
        lo = half // piece if j == 0 and d == -1 else 0
        hi = half // piece if j == 0 and d == 1 else rows // piece
        if j > 0:
            arrived(("sum", s, j - 1, other))

        def fill(begin, end, adds):
            @pl.loop(begin, end)
            def _(k):
                at = pl.multiple_of(k * piece, piece)
                value = partial(at, d * (NZ // 2 - j), other)
                if adds:
                    value += msg_in[s, j - 1, other, pl.ds(at, piece), :].astype(f32)
                msg_out[s, j, other, pl.ds(at, piece), :] = value.astype(bf16)

        if j == 1:
            mid = half // piece
            fill(0, mid, d == 1)
            fill(mid, rows // piece, d == -1)
        else:
            fill(lo, hi, j > 0)
        band = pl.ds(lo * piece, (hi - lo) * piece)
        send(("sum", s, j, other), msg_out.at[s, j, other, band], msg_in.at[s, j, other, band], z_at(d))

    for j in range(NZ // 2):
        for other in (1, 0):
            for s in (0, 1):
                message(s, j, other)

    def finish(other):
        for s in (0, 1):
            arrived(("sum", s, NZ // 2 - 1, other))

        @pl.loop(0, rows // piece)
        def _(k):
            at = pl.multiple_of(k * piece, piece)
            value = partial(at, 0, other)
            for s in (0, 1):
                value += msg_in[s, NZ // 2 - 1, other, pl.ds(at, piece), :].astype(f32)
            if other:
                y_out[pl.ds(at, piece), :] = value.astype(bf16)
            else:
                total[pl.ds(at, piece), :] = value

    finish(1)
    send("sum_y", y_out, y_in, y_far)
    finish(0)
    arrived("sum_y")
    out_ref[...] = (total[...] + y_in[...].astype(f32)).astype(bf16)
    for copy in copies.values():
        copy.wait_send()


def shards(
    tokens, in_base, in_task, feat_weight, filter_taps, decay_rates, skip_gain, out_base, out_task
):
    rows, width = tokens.shape
    chans = in_base.shape[2]
    c3 = 3 * chans
    short, longt = feat_weight.shape[0], filter_taps.shape[0]
    in_weight = (in_base.astype(f32) - in_task.astype(f32)).astype(bf16)
    in_weight = in_weight.reshape(2, 2, width, c3)
    out_weight = (out_base.astype(f32) - out_task.astype(f32)).astype(bf16)
    out_weight = out_weight.reshape(chans, 2, 2, width).transpose(1, 2, 0, 3)
    steps = NZ // 2
    vm = pltpu.VMEM
    count = 96
    return pl.pallas_call(
        functools.partial(kernel, rows, width, chans, short, longt),
        out_shape=jax.ShapeDtypeStruct((rows, width), bf16),
        in_specs=[pl.BlockSpec(memory_space=vm)] * 7,
        out_specs=pl.BlockSpec(memory_space=vm),
        scratch_shapes=[
            vm((NQ, rows, width), bf16),
            vm((NQ, width, 2 * c3), bf16),
            vm((NQ, 2 * chans, width), bf16),
            vm((rows, 2 * c3), f32),
            vm((rows, c3), f32),
            vm((HALO, c3), bf16),
            vm((HALO, c3), bf16),
            vm((HALO + rows, c3), f32),
            vm((HALO + rows, chans), f32),
            vm((8, HALO + rows, chans), f32),
            vm((rows, chans), f32),
            vm((longt, chans), f32),
            vm((rows, 2 * chans), bf16),
            vm((2, steps, 2, rows, width), bf16),
            vm((2, steps, 2, rows, width), bf16),
            vm((rows, width), bf16),
            vm((rows, width), bf16),
            vm((rows, width), f32),
            pltpu.SemaphoreType.DMA((count,)),
            pltpu.SemaphoreType.DMA((count,)),
            pltpu.SemaphoreType.DMA((3,)),
        ],
        compiler_params=pltpu.CompilerParams(
            collective_id=0, has_side_effects=True, vmem_limit_bytes=60 * 1024 * 1024
        ),
    )(
        tokens, in_weight, out_weight, feat_weight.reshape(short, c3), filter_taps,
        decay_rates.reshape(1, chans), skip_gain.reshape(1, chans),
    )


def solution(mesh):
    in_specs = (
        P("ctx", "chan"),
        P("ctx", None, "chan"),
        P("ctx", None, "chan"),
        P(None, None, "chan"),
        P(None, "chan"),
        P("chan"),
        P("chan"),
        P("chan", "ctx"),
        P("chan", "ctx"),
    )
    out_specs = P("ctx", "chan")
    return jax.shard_map(shards, mesh=mesh, in_specs=in_specs, out_specs=out_specs, check_vma=False)
```

```python
import functools

import jax
import jax.numpy as jnp
from jax import lax
from jax.experimental import pallas as pl
from jax.experimental.pallas import tpu as pltpu
from jax.sharding import PartitionSpec as P

MESH = pl.DeviceIdType.MESH
NX, NZ = 4, 8
NCTX = 2 * NX
NQ = 2 * NZ
HALO = 144
bf16, f32 = jnp.bfloat16, jnp.float32


def kernel(
    rows, width, chans, short, longt,
    tok_ref, base_ref, task_ref, obase_ref, otask_ref, feat_ref, taps_ref, decay_ref, skip_ref,
    total, y_in,
    base, task, obase, otask, w_twin, wo_twin, tok_all, w_all, wo_all, acc, part_in, halo_out, halo_in, proj, gate, shifts, query, filt,
    gated, msg_out, msg_in, y_out,
    send_sems, recv_sems, local_sems,
):
    ctx, chan = lax.axis_index("ctx"), lax.axis_index("chan")
    x, yl = ctx // 2, ctx % 2
    q, core = chan // 2, chan % 2
    yh, z = q // NZ, q % NZ
    c3 = 3 * chans

    def x_at(d):
        return ((x + d + NX) % NX) * 2 + yl, chan

    def z_at(d):
        return ctx, (yh * NZ + (z + d + NZ) % NZ) * 2 + core

    y_pair = (x * 2 + 1 - yl, chan)
    y_far = (ctx, ((1 - yh) * NZ + z) * 2 + core)
    twin = (ctx, 2 * q + 1 - core)
    after, before = ((ctx + 1) % NCTX, chan), ((ctx + NCTX - 1) % NCTX, chan)

    local = [
        pltpu.make_async_copy(src, dst, local_sems.at[k])
        for k, (src, dst) in enumerate(
            [(base_ref, base), (task_ref, task), (obase_ref, obase), (otask_ref, otask), (tok_ref, tok_all.at[q])]
        )
    ]
    for copy in local:
        copy.start()

    barrier = pltpu.get_barrier_semaphore()
    greeted = [twin, y_pair, y_far, x_at(1), x_at(-1), z_at(1), z_at(-1), after, before]
    for device in greeted:
        pl.semaphore_signal(barrier, inc=1, device_id=device, device_id_type=MESH)
    pl.semaphore_wait(barrier, len(greeted))

    copies = {}

    def send(name, src, dst, device):
        k = len(copies)
        copy = pltpu.make_async_remote_copy(
            src_ref=src, dst_ref=dst, send_sem=send_sems.at[k], recv_sem=recv_sems.at[k],
            device_id=device, device_id_type=MESH,
        )
        copy.start()
        copies[name] = copy

    def arrived(name):
        copies[name].wait_recv()

    def w_at(i, h):
        return w_all.at[pl.ds(2 * i, 2), h]

    def wo_at(i, h):
        return wo_all.at[pl.ds(2 * i, 2), pl.ds(h * chans, chans), :]

    def ctx_of(d, other):
        return ((x + d + NX) % NX) * 2 + (1 - yl if other else yl)

    def tok_at(d, other):
        return tok_all.at[(1 - yh if other else yh) * NZ + (z + d + NZ) % NZ]

    for d in (1, -1):
        send(("tok", 0, d, 1), tok_ref, tok_at(0, 0), z_at(d))
    send("tok_y", tok_ref, tok_at(0, 0), y_far)

    def less(one, two):
        return (one.astype(f32) - two.astype(f32)).astype(bf16)

    local[0].wait()
    local[1].wait()
    for owner in (1 - core, core):
        is_twin = owner is not core
        for b in range(2):
            @pl.loop(0, 3)
            def _(s):
                band = pl.ds(pl.multiple_of((2 * b + owner) * width, width), width)
                value = less(base[s, band, :], task[s, band, :])
                if is_twin:
                    w_twin[b, s] = value
                else:
                    w_all[2 * ctx + b, 0, s] = value

    send("twin_w", w_twin, w_at(ctx, 1), twin)
    for d in (1, -1):
        send(("w", 0, 0, d), w_at(ctx, 0), w_at(ctx, 0), x_at(d))
    send(("wy", 0), w_at(ctx, 0), w_at(ctx, 0), y_pair)
    local[2].wait()
    local[3].wait()
    for owner in (1 - core, core):
        is_twin = owner is not core
        for b in range(2):
            band = pl.ds(pl.multiple_of((2 * b + owner) * width, width), width)
            value = less(obase[:, band], otask[:, band])
            if is_twin:
                wo_twin[b] = value
            else:
                wo_all[2 * ctx + b, pl.ds(0, chans), :] = value
    send("twin_wo", wo_twin, wo_at(ctx, 1), twin)

    arrived("twin_w")
    for d in (1, -1):
        send(("w", 0, 1, d), w_at(ctx, 1), w_at(ctx, 1), x_at(d))
    send(("wy", 1), w_at(ctx, 1), w_at(ctx, 1), y_pair)
    local[4].wait()
    arrived("twin_wo")
    for h in (0, 1):
        send(("woy", 0, h), wo_at(ctx, h), wo_at(ctx, h), y_pair)

    lags = lax.broadcasted_iota(jnp.int32, (longt, chans), 0).astype(f32)
    filt[...] = taps_ref[...] * jnp.exp(-decay_ref[...] * lags)
    acc[...] = jnp.zeros_like(acc)

    half = rows // 2

    def tok_step(o, step):
        for d in (1, -1):
            if step == 1:
                if not o:
                    continue
                src = tok_at(0, 1)
            else:
                arrived(("tok", o, d, step - 1))
                src = tok_at(-d * (step - 1), o)
            if step == NZ // 2:
                src = src.at[pl.ds(0 if d == 1 else half, half)]
            send(("tok", o, d, step), src, src, z_at(d))

    def w_pass(o):
        for d, h in ((1, 0), (-1, 1)):
            arrived(("w", o, h, d))
            src = w_at(ctx_of(-d, o), h)
            send(("w_far", o, d), src, src, x_at(d))

    def w_second(h):
        arrived(("wy", h))
        for d in (1, -1):
            src = w_at(ctx_of(0, 1), h)
            send(("w", 1, h, d), src, src, x_at(d))

    arrived("tok_y")
    tok_step(1, 1)
    tok_step(0, 2)
    w_second(0)
    tok_step(1, 2)
    tok_step(0, 3)
    w_second(1)
    w_pass(0)
    tok_step(1, 3)
    tok_step(0, 4)
    tok_step(1, 4)
    w_pass(1)
    for h in (0, 1):
        for d in (1, -1):
            send(("wo", h, d), wo_at(ctx, h), wo_at(ctx, h), x_at(d))
    for o in (0, 1):
        for d in (1, -1):
            arrived(("tok", o, d, NZ // 2))
            arrived(("w", o, 1 if d == 1 else 0, d))

    def accumulate(k, first, size):
        i = ((x + k // 2 + NX - 1) % NX) * 2 + k % 2
        cols = pl.ds(first, size)

        def weights(k):
            parts = [divmod(t, 3) for t in range(first // chans, (first + size) // chans)]
            return jnp.concatenate([w_all[k, h, s] for h, s in parts], axis=1)

        for r in range(2):
            band = pl.ds(r * half, half)
            acc[band, cols] += jnp.dot(
                tok_all[2 * i, band, :], weights(2 * i), preferred_element_type=f32
            ) + jnp.dot(
                tok_all[2 * i + 1, band, :], weights(2 * i + 1), preferred_element_type=f32
            )

    @pl.loop(0, 2 * NX - 2)
    def _(k):
        accumulate(k, 0, 2 * c3)

    for o in (0, 1):
        for d in (1, -1):
            arrived(("w_far", o, d))

    @pl.loop(2 * NX - 2, 2 * NX)
    def _(k):
        accumulate(k, c3, c3)

    send("part", acc.at[:, pl.ds(c3, c3)], part_in, twin)

    @pl.loop(2 * NX - 2, 2 * NX)
    def _(k):
        accumulate(k, 0, c3)

    for d in (1, -1):
        for h in (0, 1):
            arrived(("wo", h, d))
            src = wo_at(ctx_of(-d, 0), h)
            send(("woy", d, h), src, src, y_pair)
        src = wo_at(ctx_of(-d, 0), 0 if d == 1 else 1)
        send(("wo_far", d), src, src, x_at(d))

    arrived("part")
    last = pl.ds(rows - HALO, HALO)
    tail = (acc[last, pl.ds(0, c3)] + part_in[last, :]).astype(bf16)
    halo_out[...] = tail
    proj[pl.ds(rows, HALO), :] = tail.astype(f32)
    step_rows = (rows - HALO) // 2

    @pl.loop(0, 2)
    def _(k):
        at = pl.multiple_of(k * step_rows, 8)
        mine = (acc[pl.ds(at, step_rows), pl.ds(0, c3)] + part_in[pl.ds(at, step_rows), :]).astype(bf16)
        proj[pl.ds(pl.multiple_of(at + HALO, 8), step_rows), :] = mine.astype(f32)

    send("halo", halo_out, halo_in, after)

    def featurize(begin, count, with_query):
        size = 32

        @pl.loop(0, count // size)
        def _(k):
            at = pl.multiple_of(begin + k * size, 8)
            values = []
            for s in range(3):
                if s == 0 and not with_query:
                    values.append(None)
                    continue
                lanes = pl.ds(s * chans, chans)
                block = proj[pl.ds(pl.multiple_of(at - 8, 8), size + 8), lanes]
                value = feat_ref[0:1, lanes] * block[8:]
                for i in range(1, short):
                    value += feat_ref[i : i + 1, lanes] * block[8 - i : 8 - i + size]
                values.append(value)
            gate[pl.ds(at, size), :] = values[1] * values[2]
            if with_query:
                query[pl.ds(pl.multiple_of(at - HALO, 8), size), :] = values[0]

    def shift(begin, count):
        size = 32

        @pl.loop(0, count // size)
        def _(k):
            at = pl.multiple_of(begin + k * size, 8)
            block = gate[pl.ds(pl.multiple_of(at - 8, 8), size + 8), :]
            for r in range(8):
                shifts[r, pl.ds(at, size), :] = block[8 - r : 8 - r + size]

    tile = 64

    def convolve(begin, count):
        @pl.loop(begin, begin + count)
        def _(k):
            at = pl.multiple_of(k * tile, tile)
            own = shifts[0, pl.ds(pl.multiple_of(at + HALO, 8), tile), :]
            value = skip_ref[...] * own
            for j in range(longt):
                back, r = j - j % 8, j % 8
                value += filt[j : j + 1, :] * shifts[r, pl.ds(pl.multiple_of(at + HALO - back, 8), tile), :]
            gated[pl.ds(at, tile), pl.ds(0, chans)] = (query[pl.ds(at, tile), :] * value).astype(bf16)

    tiles = rows // tile
    first_free = 3
    featurize(HALO + 32, rows - 32, True)
    shift(HALO + 48, rows - 64)
    shift(HALO + rows - 32, 32)
    convolve(first_free, tiles - first_free)
    band = pl.ds(first_free * tile, rows - first_free * tile)
    send("gated_hi", gated.at[band, pl.ds(0, chans)], gated.at[band, pl.ds(chans, chans)], twin)

    for d in (1, -1):
        arrived(("wo_far", d))
        src = wo_at(ctx_of(2, 0), 0 if d == 1 else 1)
        send(("woy_far", d), src, src, y_pair)

    arrived("halo")
    proj[pl.ds(0, HALO), :] = jnp.where(ctx == 0, 0.0, halo_in[...].astype(f32))
    featurize(16, HALO - 16, False)
    featurize(HALO, 32, True)
    shift(24, HALO + 48)
    convolve(0, first_free)
    band = pl.ds(0, first_free * tile)
    send("gated_lo", gated.at[band, pl.ds(0, chans)], gated.at[band, pl.ds(chans, chans)], twin)
    for d in (1, -1):
        for h in (0, 1):
            arrived(("woy", d, h))
        arrived(("woy_far", d))
    for h in (0, 1):
        arrived(("woy", 0, h))
    arrived("gated_hi")
    arrived("gated_lo")

    piece = 128

    def partial(at, d, other):
        to = (1 - yh if other else yh) * NZ + (z + d + NZ) % NZ
        return jnp.dot(gated[pl.ds(at, piece), :], wo_all[to], preferred_element_type=f32)

    def message(s, j, other):
        d = 1 if s == 0 else -1
        lo = half // piece if j == 0 and d == -1 else 0
        hi = half // piece if j == 0 and d == 1 else rows // piece
        if j > 0:
            arrived(("sum", s, j - 1, other))

        def fill(begin, end, adds):
            @pl.loop(begin, end)
            def _(k):
                at = pl.multiple_of(k * piece, piece)
                value = partial(at, d * (NZ // 2 - j), other)
                if adds:
                    value += msg_in[s, j - 1, other, pl.ds(at, piece), :].astype(f32)
                msg_out[s, j, other, pl.ds(at, piece), :] = value.astype(bf16)

        if j == 1:
            mid = half // piece
            fill(0, mid, d == 1)
            fill(mid, rows // piece, d == -1)
        else:
            fill(lo, hi, j > 0)
        band = pl.ds(lo * piece, (hi - lo) * piece)
        send(("sum", s, j, other), msg_out.at[s, j, other, band], msg_in.at[s, j, other, band], z_at(d))

    for j in range(NZ // 2):
        for other in (1, 0):
            for s in (0, 1):
                message(s, j, other)

    def finish(other):
        for s in (0, 1):
            arrived(("sum", s, NZ // 2 - 1, other))

        @pl.loop(0, rows // piece)
        def _(k):
            at = pl.multiple_of(k * piece, piece)
            value = partial(at, 0, other)
            for s in (0, 1):
                value += msg_in[s, NZ // 2 - 1, other, pl.ds(at, piece), :].astype(f32)
            if other:
                y_out[pl.ds(at, piece), :] = value.astype(bf16)
            else:
                total[pl.ds(at, piece), :] = value

    finish(1)
    send("sum_y", y_out, y_in, y_far)
    finish(0)
    arrived("sum_y")
    for copy in copies.values():
        copy.wait_send()


def shards(
    tokens, in_base, in_task, feat_weight, filter_taps, decay_rates, skip_gain, out_base, out_task
):
    rows, width = tokens.shape
    chans = in_base.shape[2]
    c3 = 3 * chans
    short, longt = feat_weight.shape[0], filter_taps.shape[0]
    steps = NZ // 2
    vm, count = pltpu.VMEM, 96
    in_vmem, anywhere = pl.BlockSpec(memory_space=vm), pl.BlockSpec(memory_space=pl.ANY)
    total, across = pl.pallas_call(
        functools.partial(kernel, rows, width, chans, short, longt),
        out_shape=[jax.ShapeDtypeStruct((rows, width), f32), jax.ShapeDtypeStruct((rows, width), bf16)],
        in_specs=[anywhere] * 5 + [in_vmem] * 4,
        out_specs=[in_vmem] * 2,
        scratch_shapes=[
            vm((3, in_base.shape[0], chans), bf16),
            vm((3, in_base.shape[0], chans), bf16),
            vm(out_base.shape, bf16),
            vm(out_base.shape, bf16),
            vm((2, 3, width, chans), bf16),
            vm((2, chans, width), bf16),
            vm((NQ, rows, width), bf16),
            vm((NQ, 2, 3, width, chans), bf16),
            vm((NQ, 2 * chans, width), bf16),
            vm((rows, 2 * c3), f32),
            vm((rows, c3), f32),
            vm((HALO, c3), bf16),
            vm((HALO, c3), bf16),
            vm((HALO + rows, c3), f32),
            vm((HALO + rows, chans), f32),
            vm((8, HALO + rows, chans), f32),
            vm((rows, chans), f32),
            vm((longt, chans), f32),
            vm((rows, 2 * chans), bf16),
            vm((2, steps, 2, rows, width), bf16),
            vm((2, steps, 2, rows, width), bf16),
            vm((rows, width), bf16),
            pltpu.SemaphoreType.DMA((count,)),
            pltpu.SemaphoreType.DMA((count,)),
            pltpu.SemaphoreType.DMA((5,)),
        ],
        compiler_params=pltpu.CompilerParams(
            collective_id=0, has_side_effects=True, vmem_limit_bytes=60 * 1024 * 1024
        ),
    )(
        tokens, in_base.transpose(1, 0, 2), in_task.transpose(1, 0, 2), out_base, out_task,
        feat_weight.reshape(short, c3), filter_taps, decay_rates.reshape(1, chans), skip_gain.reshape(1, chans),
    )
    return (total + across.astype(f32)).astype(bf16)


def solution(mesh):
    in_specs = (
        P("ctx", "chan"),
        P("ctx", None, "chan"),
        P("ctx", None, "chan"),
        P(None, None, "chan"),
        P(None, "chan"),
        P("chan"),
        P("chan"),
        P("chan", "ctx"),
        P("chan", "ctx"),
    )
    out_specs = P("ctx", "chan")
    return jax.shard_map(shards, mesh=mesh, in_specs=in_specs, out_specs=out_specs, check_vma=False)
```

```python
import functools

import jax
import jax.numpy as jnp
from jax import lax
from jax.experimental import pallas as pl
from jax.experimental.pallas import tpu as pltpu
from jax.sharding import PartitionSpec as P

MESH = pl.DeviceIdType.MESH
NX, NZ = 4, 8
NCTX = 2 * NX
NQ = 2 * NZ
HALO = 144
bf16, f32 = jnp.bfloat16, jnp.float32


def kernel(
    rows, width, chans, short, longt,
    tok_ref, base_ref, task_ref, obase_ref, otask_ref, feat_ref, taps_ref, decay_ref, skip_ref,
    out_ref,
    base, task, obase, otask, w_twin, wo_twin, tok_all, w_all, wo_all, acc, part_in, halo_out, halo_in, proj, gate, shifts, query, filt,
    gated, msg_out, msg_in, first_out, first_in, y_out, y_in, total,
    send_sems, recv_sems, local_sems,
):
    ctx, chan = lax.axis_index("ctx"), lax.axis_index("chan")
    x, yl = ctx // 2, ctx % 2
    q, core = chan // 2, chan % 2
    yh, z = q // NZ, q % NZ
    c3 = 3 * chans

    def x_at(d):
        return ((x + d + NX) % NX) * 2 + yl, chan

    def z_at(d):
        return ctx, (yh * NZ + (z + d + NZ) % NZ) * 2 + core

    y_pair = (x * 2 + 1 - yl, chan)
    y_far = (ctx, ((1 - yh) * NZ + z) * 2 + core)
    twin = (ctx, 2 * q + 1 - core)
    after, before = ((ctx + 1) % NCTX, chan), ((ctx + NCTX - 1) % NCTX, chan)

    local = [
        pltpu.make_async_copy(src, dst, local_sems.at[k])
        for k, (src, dst) in enumerate(
            [(base_ref, base), (task_ref, task), (obase_ref, obase), (otask_ref, otask), (tok_ref, tok_all.at[q])]
        )
    ]
    for copy in local:
        copy.start()

    barrier = pltpu.get_barrier_semaphore()
    greeted = [twin, y_pair, y_far, x_at(1), x_at(-1), z_at(1), z_at(-1), after, before]
    for device in greeted:
        pl.semaphore_signal(barrier, inc=1, device_id=device, device_id_type=MESH)
    pl.semaphore_wait(barrier, len(greeted))

    copies = {}

    def send(name, src, dst, device):
        k = len(copies)
        copy = pltpu.make_async_remote_copy(
            src_ref=src, dst_ref=dst, send_sem=send_sems.at[k], recv_sem=recv_sems.at[k],
            device_id=device, device_id_type=MESH,
        )
        copy.start()
        copies[name] = copy

    def arrived(name):
        copies[name].wait_recv()

    def w_at(i, h, begin=0, end=3):
        return w_all.at[pl.ds(2 * i, 2), h, pl.ds(begin, end - begin)]

    def wo_at(i, h):
        return wo_all.at[pl.ds(2 * i, 2), pl.ds(h * chans, chans), :]

    def ctx_of(d, other):
        return ((x + d + NX) % NX) * 2 + (1 - yl if other else yl)

    def tok_at(d, other):
        return tok_all.at[(1 - yh if other else yh) * NZ + (z + d + NZ) % NZ]

    for d in (1, -1):
        send(("tok", 0, d, 1), tok_ref, tok_at(0, 0), z_at(d))
    send("tok_y", tok_ref, tok_at(0, 0), y_far)

    def less(one, two):
        return (one.astype(f32) - two.astype(f32)).astype(bf16)

    local[0].wait()
    local[1].wait()
    for owner in (1 - core, core):
        is_twin = owner is not core
        for b in range(2):
            @pl.loop(0, 3)
            def _(s):
                band = pl.ds(pl.multiple_of((2 * b + owner) * width, width), width)
                value = less(base[s, band, :], task[s, band, :])
                if is_twin:
                    w_twin[b, s] = value
                else:
                    w_all[2 * ctx + b, 0, s] = value

    send("twin_w", w_twin, w_at(ctx, 1), twin)
    for d in (1, -1):
        send(("w", 0, 0, d), w_at(ctx, 0), w_at(ctx, 0), x_at(d))
    send(("wy", 0), w_at(ctx, 0), w_at(ctx, 0), y_pair)
    local[2].wait()
    local[3].wait()
    for owner in (1 - core, core):
        is_twin = owner is not core
        for b in range(2):
            band = pl.ds(pl.multiple_of((2 * b + owner) * width, width), width)
            value = less(obase[:, band], otask[:, band])
            if is_twin:
                wo_twin[b] = value
            else:
                wo_all[2 * ctx + b, pl.ds(0, chans), :] = value
    send("twin_wo", wo_twin, wo_at(ctx, 1), twin)

    arrived("twin_w")
    for d in (1, -1):
        send(("w", 0, 1, d), w_at(ctx, 1), w_at(ctx, 1), x_at(d))
    send(("wy", 1), w_at(ctx, 1), w_at(ctx, 1), y_pair)
    local[4].wait()
    arrived("twin_wo")
    send(("woy", 0), wo_at(ctx, 0), wo_at(ctx, 0), y_pair)

    lags = lax.broadcasted_iota(jnp.int32, (longt, chans), 0).astype(f32)
    filt[...] = taps_ref[...] * jnp.exp(-decay_ref[...] * lags)
    acc[...] = jnp.zeros_like(acc)

    half = rows // 2

    def tok_step(o, step):
        for d in (1, -1):
            if step == 1:
                if not o:
                    continue
                src = tok_at(0, 1)
            else:
                arrived(("tok", o, d, step - 1))
                src = tok_at(-d * (step - 1), o)
            if step == NZ // 2:
                src = src.at[pl.ds(0 if d == 1 else half, half)]
            send(("tok", o, d, step), src, src, z_at(d))

    way = {1: 0, -1: 1}

    def w_first(h):
        for d in (1, -1):
            arrived(("w", 0, h, d))
            src = w_at(ctx_of(-d, 0), h)
            if way[d] == h:
                send(("w_far", 0, d), src, src, x_at(d))
            src = w_at(ctx_of(-d, 0), h, 2, 3)
            send(("wy", d, h), src, src, y_pair)

    def w_second(h):
        arrived(("wy", h))
        for d in (1, -1):
            src = w_at(ctx_of(0, 1), h, 0, 2)
            send(("w", 1, h, d), src, src, x_at(d))

    def w_third(h):
        for d in (1, -1):
            arrived(("w", 1, h, d))
            if way[d] == h:
                src = w_at(ctx_of(-d, 1), h, 0, 2)
                send(("w_far", 1, d), src, src, x_at(d))

    def w_last():
        for d in (1, -1):
            arrived(("w_far", 0, d))
            src = w_at(ctx_of(2, 0), way[d], 2, 3)
            send(("wy_far", d), src, src, y_pair)

    arrived("tok_y")
    tok_step(1, 1)
    tok_step(0, 2)
    w_first(0)
    w_second(0)
    tok_step(1, 2)
    tok_step(0, 3)
    w_first(1)
    w_second(1)
    tok_step(1, 3)
    w_last()
    send(("woy", 1), wo_at(ctx, 1), wo_at(ctx, 1), y_pair)
    tok_step(0, 4)
    w_third(0)
    tok_step(1, 4)
    w_third(1)
    for h in (0, 1):
        for d in (1, -1):
            send(("wo", 0, h, d), wo_at(ctx, h), wo_at(ctx, h), x_at(d))
    arrived(("woy", 0))
    for d in (1, -1):
        src = wo_at(ctx_of(0, 1), 0)
        send(("wo", 1, 0, d), src, src, x_at(d))
    for o in (0, 1):
        for d in (1, -1):
            arrived(("tok", o, d, NZ // 2))
    for d in (1, -1):
        for h in (0, 1):
            arrived(("wy", d, h))

    def accumulate(k, first, size):
        i = ((x + k // 2 + NX - 1) % NX) * 2 + k % 2
        cols = pl.ds(first, size)

        def weights(k):
            parts = [divmod(t, 3) for t in range(first // chans, (first + size) // chans)]
            return jnp.concatenate([w_all[k, h, s] for h, s in parts], axis=1)

        for r in range(2):
            band = pl.ds(r * half, half)
            acc[band, cols] += jnp.dot(
                tok_all[2 * i, band, :], weights(2 * i), preferred_element_type=f32
            ) + jnp.dot(
                tok_all[2 * i + 1, band, :], weights(2 * i + 1), preferred_element_type=f32
            )

    @pl.loop(0, 2 * NX - 2)
    def _(k):
        accumulate(k, 0, 2 * c3)

    for d in (1, -1):
        arrived(("w_far", 1, d))
        arrived(("wy_far", d))

    @pl.loop(2 * NX - 2, 2 * NX)
    def _(k):
        accumulate(k, c3, c3)

    send("part", acc.at[:, pl.ds(c3, c3)], part_in, twin)

    @pl.loop(2 * NX - 2, 2 * NX)
    def _(k):
        accumulate(k, 0, c3)

    def wo_pass():
        for h in (1, 0):
            for d in (1, -1):
                arrived(("wo", 0, h, d))
                src = wo_at(ctx_of(-d, 0), h)
                if way[d] == h:
                    send(("wo_far", 0, d), src, src, x_at(d))
                if h == 1:
                    send(("wo_y", d), src, src, y_pair)
        for d in (1, -1):
            arrived(("wo", 1, 0, d))
            src = wo_all.at[2 * ctx_of(-d, 1) + way[d], pl.ds(0, chans), :]
            send(("wo_far", 1, d), src, src, x_at(d))

    def wo_last():
        arrived(("wo_far", 0, -1))
        src = wo_at(ctx_of(2, 0), 1)
        send("wo_y_far", src, src, y_pair)

    arrived("part")
    last = pl.ds(rows - HALO, HALO)
    tail = (acc[last, pl.ds(0, c3)] + part_in[last, :]).astype(bf16)
    halo_out[...] = tail
    proj[pl.ds(rows, HALO), :] = tail.astype(f32)
    step_rows = (rows - HALO) // 2

    @pl.loop(0, 2)
    def _(k):
        at = pl.multiple_of(k * step_rows, 8)
        mine = (acc[pl.ds(at, step_rows), pl.ds(0, c3)] + part_in[pl.ds(at, step_rows), :]).astype(bf16)
        proj[pl.ds(pl.multiple_of(at + HALO, 8), step_rows), :] = mine.astype(f32)

    send("halo", halo_out, halo_in, after)

    def featurize(begin, count, with_query):
        size = 32

        @pl.loop(0, count // size)
        def _(k):
            at = pl.multiple_of(begin + k * size, 8)
            values = []
            for s in range(3):
                if s == 0 and not with_query:
                    values.append(None)
                    continue
                lanes = pl.ds(s * chans, chans)
                block = proj[pl.ds(pl.multiple_of(at - 8, 8), size + 8), lanes]
                value = feat_ref[0:1, lanes] * block[8:]
                for i in range(1, short):
                    value += feat_ref[i : i + 1, lanes] * block[8 - i : 8 - i + size]
                values.append(value)
            gate[pl.ds(at, size), :] = values[1] * values[2]
            if with_query:
                query[pl.ds(pl.multiple_of(at - HALO, 8), size), :] = values[0]

    def shift(begin, count):
        size = 32

        @pl.loop(0, count // size)
        def _(k):
            at = pl.multiple_of(begin + k * size, 8)
            block = gate[pl.ds(pl.multiple_of(at - 8, 8), size + 8), :]
            for r in range(8):
                shifts[r, pl.ds(at, size), :] = block[8 - r : 8 - r + size]

    tile = 64

    def convolve(begin, count):
        @pl.loop(begin, begin + count)
        def _(k):
            at = pl.multiple_of(k * tile, tile)
            own = shifts[0, pl.ds(pl.multiple_of(at + HALO, 8), tile), :]
            value = skip_ref[...] * own
            for j in range(longt):
                back, r = j - j % 8, j % 8
                value += filt[j : j + 1, :] * shifts[r, pl.ds(pl.multiple_of(at + HALO - back, 8), tile), :]
            gated[pl.ds(at, tile), pl.ds(0, chans)] = (query[pl.ds(at, tile), :] * value).astype(bf16)

    tiles = half // tile
    upper = HALO + half - 112
    featurize(upper - 48, HALO + rows - upper + 48, True)
    shift(upper - 16, HALO + rows - upper + 16)
    convolve(tiles, tiles)
    band = pl.ds(half, half)
    send("gated_hi", gated.at[band, pl.ds(0, chans)], gated.at[band, pl.ds(chans, chans)], twin)
    wo_pass()

    arrived("halo")
    proj[pl.ds(0, HALO), :] = jnp.where(ctx == 0, 0.0, halo_in[...].astype(f32))
    featurize(16, HALO - 16, False)
    featurize(HALO, upper - 48 - HALO, True)
    shift(24, upper - 32)
    convolve(0, tiles)
    band = pl.ds(0, half)
    send("gated_lo", gated.at[band, pl.ds(0, chans)], gated.at[band, pl.ds(chans, chans)], twin)
    wo_last()
    for d in (1, -1):
        arrived(("wo_y", d))
        arrived(("wo_far", 1, d))
    arrived(("wo_far", 0, 1))
    arrived(("woy", 1))
    arrived("wo_y_far")
    arrived("gated_hi")

    piece = half // 2
    order = [4, 3, -3, 2, -2, 1, -1, 0]

    def partial(at, d, other):
        to = (1 - yh if other else yh) * NZ + (z + d + NZ) % NZ
        return jnp.dot(gated[pl.ds(at, piece), :], wo_all[to], preferred_element_type=f32)

    def part(p):
        return pl.ds(pl.multiple_of(p * piece, piece), piece)

    def base_row(kind):
        return 0 if kind == 2 else half

    def message(kind, j):
        for s, d in enumerate((1, -1)):
            if j > 0:
                arrived(("sum", kind, s, j - 1))
            slot = order.index(abs(4 - j) if j == 0 else d * (4 - j))
            if kind == 2 and (j > 0 or s == 0):
                arrived(("first", slot))
            pieces = (way[d],) if j == 0 else (0, 1)
            for p in pieces:
                value = partial(base_row(kind) + p * piece, d * (4 - j), kind == 0)
                if kind == 2:
                    value += first_in[slot, part(p), :].astype(f32)
                if j > 1 or (j == 1 and p == way[d]):
                    value += msg_in[s, j - 1, kind, part(p), :].astype(f32)
                msg_out[s, j, kind, part(p), :] = value.astype(bf16)
            band = pl.ds(pieces[0] * piece, len(pieces) * piece)
            send(("sum", kind, s, j), msg_out.at[s, j, kind, band], msg_in.at[s, j, kind, band], z_at(d))

    def finish(kind):
        for s in (0, 1):
            arrived(("sum", kind, s, 3))
        if kind == 2:
            arrived(("first", order.index(0)))
        for p in (0, 1):
            value = partial(base_row(kind) + p * piece, 0, kind == 0)
            for s in (0, 1):
                value += msg_in[s, 3, kind, part(p), :].astype(f32)
            if kind == 0:
                y_out[part(p), :] = value.astype(bf16)
            elif kind == 1:
                total[part(p), :] = value
            else:
                value += first_in[order.index(0), part(p), :].astype(f32)
                out_ref[part(p), :] = value.astype(bf16)

    message(0, 0)
    message(1, 0)
    arrived("gated_lo")
    for slot, d in enumerate(order):
        for p in (0, 1):
            first_out[slot, part(p), :] = partial(p * piece, d, True).astype(bf16)
        send(("first", slot), first_out.at[slot], first_in.at[slot], y_far)
    for kind, j in [(0, 1), (2, 0), (1, 1), (0, 2), (2, 1), (1, 2), (0, 3), (2, 2), (1, 3)]:
        message(kind, j)
    finish(0)
    send("sum_y", y_out, y_in, y_far)
    message(2, 3)
    finish(1)
    finish(2)
    arrived("sum_y")
    out_ref[pl.ds(half, half), :] = (total[...] + y_in[...].astype(f32)).astype(bf16)
    for copy in copies.values():
        copy.wait_send()


def shards(
    tokens, in_base, in_task, feat_weight, filter_taps, decay_rates, skip_gain, out_base, out_task
):
    rows, width = tokens.shape
    chans = in_base.shape[2]
    c3 = 3 * chans
    short, longt = feat_weight.shape[0], filter_taps.shape[0]
    vm, count = pltpu.VMEM, 96
    in_vmem, anywhere = pl.BlockSpec(memory_space=vm), pl.BlockSpec(memory_space=pl.ANY)
    return pl.pallas_call(
        functools.partial(kernel, rows, width, chans, short, longt),
        out_shape=jax.ShapeDtypeStruct((rows, width), bf16),
        in_specs=[anywhere] * 5 + [in_vmem] * 4,
        out_specs=in_vmem,
        scratch_shapes=[
            vm((3, in_base.shape[0], chans), bf16),
            vm((3, in_base.shape[0], chans), bf16),
            vm(out_base.shape, bf16),
            vm(out_base.shape, bf16),
            vm((2, 3, width, chans), bf16),
            vm((2, chans, width), bf16),
            vm((NQ, rows, width), bf16),
            vm((NQ, 2, 3, width, chans), bf16),
            vm((NQ, 2 * chans, width), bf16),
            vm((rows, 2 * c3), f32),
            vm((rows, c3), f32),
            vm((HALO, c3), bf16),
            vm((HALO, c3), bf16),
            vm((HALO + rows, c3), f32),
            vm((HALO + rows, chans), f32),
            vm((8, HALO + rows, chans), f32),
            vm((rows, chans), f32),
            vm((longt, chans), f32),
            vm((rows, 2 * chans), bf16),
            vm((2, NZ // 2, 3, rows // 2, width), bf16),
            vm((2, NZ // 2, 3, rows // 2, width), bf16),
            vm((NZ, rows // 2, width), bf16),
            vm((NZ, rows // 2, width), bf16),
            vm((rows // 2, width), bf16),
            vm((rows // 2, width), bf16),
            vm((rows // 2, width), f32),
            pltpu.SemaphoreType.DMA((count,)),
            pltpu.SemaphoreType.DMA((count,)),
            pltpu.SemaphoreType.DMA((5,)),
        ],
        compiler_params=pltpu.CompilerParams(
            collective_id=0, has_side_effects=True, vmem_limit_bytes=60 * 1024 * 1024
        ),
    )(
        tokens, in_base.transpose(1, 0, 2), in_task.transpose(1, 0, 2), out_base, out_task,
        feat_weight.reshape(short, c3), filter_taps, decay_rates.reshape(1, chans), skip_gain.reshape(1, chans),
    )


def solution(mesh):
    in_specs = (
        P("ctx", "chan"),
        P("ctx", None, "chan"),
        P("ctx", None, "chan"),
        P(None, None, "chan"),
        P(None, "chan"),
        P("chan"),
        P("chan"),
        P("chan", "ctx"),
        P("chan", "ctx"),
    )
    out_specs = P("ctx", "chan")
    return jax.shard_map(shards, mesh=mesh, in_specs=in_specs, out_specs=out_specs, check_vma=False)
```
